32 devices in a mesh: ctx: 4 (over z), exp: 4 (over y, x), head: 2 (over core).
Axes of the slice: x: 2, y: 2, z: 4, core: 2. Of those that a mesh axis runs over, the one named last changes fastest.
Arguments:
- queries: bfloat16 [2048, 2048], P(('ctx', 'exp'), 'head'), may hold values from -6 to 6
- keys: bfloat16 [2048, 256], P(('ctx', 'exp'), 'head'), may hold values from -6 to 6
- values: bfloat16 [2048, 256], P(('ctx', 'exp'), 'head'), may hold values from -12 to 12
- residual: bfloat16 [2048, 2880], P(('ctx', 'exp', 'head')), may hold values from -48 to 48
- out_projection: bfloat16 [2048, 2880], P('head', 'exp'), may hold values from -0.125 to 0.125
- norm_gain: float32 [2880], replicated, may hold values from 0.25 to 1.75
- route_ids: int32 [2048, 4], P(('ctx', 'exp', 'head')), may hold values from 0 to 7, all different within a row; in each aligned block of 64 rows (0 to 63, 64 to 127, ...) at most 64 rows name the same one
- route_weights: float32 [2048, 4], P(('ctx', 'exp', 'head')), may hold values from 0.05 to 1
- w_gate: bfloat16 [8, 2880, 1536], P(('ctx', 'head'), None, 'exp'), may hold values from -0.109375 to 0.109375
- w_up: bfloat16 [8, 2880, 1536], P(('ctx', 'head'), None, 'exp'), may hold values from -0.109375 to 0.109375
- w_down: bfloat16 [8, 1536, 2880], P(('ctx', 'head'), 'exp'), may hold values from -0.15625 to 0.15625
Outputs:
- mixed: bfloat16 [2048, 2880], P(('ctx', 'exp', 'head'))
The draws below stay inside these ranges and needn't reach their ends.
Inputs may be any that keep to these rules, and one draw needn't show every extreme that they name: `route_ids`: each row names 4 different experts. In the rows of one device (aligned blocks of 64 rows) no expert is named by more than 64 rows, a bound that some block reaches.
All inputs are finite; a program needn't handle non-finite values.
Results may differ from the reference program's by a relative error of at most 0.0037.
Values may be sent and summed in bfloat16 or wider, within the bound.
No kernel may reach another device: no remote copies, remote signals or barrier semaphores. Data moves between devices by JAX's collectives and lax.ppermute only.
A program may use at most 128 MiB of HBM per device.

```python
import math
import jax
import jax.numpy as jnp
import numpy as np
from jax import lax

D = 2880
QUERY_HEADS = 32
KEY_VALUE_HEADS = 4
HEAD_DIMENSION = 64
BAND_WIDTH_KEYS = 128
HID = 1536
TOP = 4
TOK_DEV = 128
SEQUENCE_TOKENS = 2048
EXPERTS = 8
CAP = 64
N_HEAD = 2


def draw_queries(key, part):
    draw_key = jax.random.fold_in(key, 303)
    value_start = jax.random.truncated_normal(draw_key, -6.0, 6.0, (SEQUENCE_TOKENS, QUERY_HEADS, HEAD_DIMENSION), jnp.float32)
    return value_start.reshape(SEQUENCE_TOKENS, QUERY_HEADS * HEAD_DIMENSION).astype(jnp.bfloat16)


def draw_keys(key, part):
    draw_key = jax.random.fold_in(key, 304)
    value_start = jax.random.truncated_normal(draw_key, -6.0, 6.0, (SEQUENCE_TOKENS, KEY_VALUE_HEADS, HEAD_DIMENSION), jnp.float32)
    return value_start.reshape(SEQUENCE_TOKENS, KEY_VALUE_HEADS * HEAD_DIMENSION).astype(jnp.bfloat16)


def draw_residual(key, part):
    base_key = jax.random.fold_in(key, 311)
    row_key = jax.random.fold_in(key, 312)
    column_key = jax.random.fold_in(key, 313)
    base = jax.random.truncated_normal(base_key, -4.0, 4.0, (SEQUENCE_TOKENS, D), jnp.float32)
    row_scale = jnp.exp(jax.random.uniform(row_key, (SEQUENCE_TOKENS, 1), jnp.float32, math.log(0.3), math.log(3.0)))
    column_scale = jnp.exp(jax.random.uniform(column_key, (1, D), jnp.float32, math.log(0.3), math.log(3.0)))
    return (base * row_scale * column_scale).astype(jnp.bfloat16)


def block_scale(rng, dims, cuts, low, high):
    factor_of, own = 1.0, jax.random.fold_in(rng, 6)
    for dim, parts in cuts:
        draws = jnp.exp(jax.random.uniform(jax.random.fold_in(own, dim), (parts,), jnp.float32, low / len(cuts), high / len(cuts)))
        factor_of = factor_of * jnp.repeat(draws, dims[dim] // parts).reshape([-1 if axis == dim else 1 for axis in range(len(dims))])
    return factor_of


def assign_block(own_key, own, number, rows, amount, top, limit, lean):
    sequence = jax.random.permutation(own_key, amount)
    crowded, usual = portions_of(amount, rows * top, limit, lean, True), portions_of(amount, rows * top, limit, lean, False)
    places = jnp.arange(amount)

    def named(sizes, rotation):
        used = int((sizes > 0).sum())
        fixed = max(1, used // 4)
        passed = fixed + (places - fixed + rotation * (used - fixed)) % max(1, amount - fixed)
        return jnp.zeros((amount,), jnp.int32).at[sequence[jnp.where(places < fixed, places, passed)]].set(jnp.asarray(sizes, jnp.int32))

    sizes = jnp.where(number % 4 == 0, named(crowded, number // 4), named(usual, number - number // 4 - 1))
    mixed = jax.random.permutation(jax.random.fold_in(own, 3), amount)
    donor, taker = mixed[0:amount // 2 * 2:2], mixed[1:amount // 2 * 2:2]
    room = jnp.minimum(sizes[donor] - 1, limit - sizes[taker]) // 2
    room = jnp.where((donor == sequence[0]) | (taker == sequence[0]) | (sizes[taker] == 0), 0, jnp.maximum(room, 0))
    passed = jax.random.randint(jax.random.fold_in(own, 4), (amount // 2,), 0, 1 << 20) % (room + 1)
    sizes = sizes.at[donor].add(-passed).at[taker].add(passed)
    items = jnp.searchsorted(jnp.cumsum(sizes), jnp.arange(rows * top), side="right").astype(jnp.int32)
    grid = items.reshape(top, rows).T
    grid = grid[jax.random.permutation(jax.random.fold_in(own, 1), rows)]
    rotation = jax.random.randint(jax.random.fold_in(own, 2), (rows, 1), 0, top)
    return jnp.take_along_axis(grid, (jnp.arange(top)[None, :] + rotation) % top, axis=1)


def portions_of(number_of, total, limit, skew, full):
    weights = [(1 << 20) // math.isqrt(grade ** skew) + 1 for grade in range(1, number_of + 1)]
    largest = limit if full else min(limit, max(-(-total // number_of), total * weights[0] // sum(weights)))
    least = 1 if total - largest >= number_of - 1 else 0
    given, spare = [largest] + [least] * (number_of - 1), total - largest - least * (number_of - 1)
    while spare > 0:
        candidates = [i for i in range(1, number_of) if given[i] < largest] or [i for i in range(1, number_of) if given[i] < limit]
        mass, remaining = sum([weights[i] for i in candidates]), spare
        for i in candidates:
            more = min(limit - given[i], max(1, remaining * weights[i] // mass), spare)
            given[i] = given[i] + more
            spare = spare - more
    return np.array(given)


def scatter_about(rng, dims, width, limit, cuts=(), held_as=jnp.bfloat16):
    factor_of = block_scale(rng, dims, cuts, -0.22, 0.18) if cuts else 1.0
    values = jax.random.normal(rng, dims, jnp.float32) * width * factor_of
    return jnp.minimum(jnp.maximum(values, -limit), limit).astype(held_as)


def setup_inputs(seed: int = 0) -> dict:
    key_of = jax.random.split(jax.random.key(seed), 12)
    queries = draw_queries(jax.random.fold_in(key_of[11], 71), 0)
    keys = draw_keys(jax.random.fold_in(key_of[11], 71), 0)
    values = scatter_about(key_of[2], (SEQUENCE_TOKENS, KEY_VALUE_HEADS * HEAD_DIMENSION), 2.0, 12.0, ((0, 16), (1, 2)))
    residual = draw_residual(jax.random.fold_in(key_of[11], 71), 0)
    out_projection = scatter_about(key_of[4], (QUERY_HEADS * HEAD_DIMENSION, D), (QUERY_HEADS * HEAD_DIMENSION) ** -0.5, 0.125, ((0, 2), (1, 4)))
    norm_gain = jnp.clip(1.0 + 0.15 * jax.random.normal(key_of[5], (D,), jnp.float32), 0.25, 1.75)
    route_ids_keys = jax.random.split(jax.random.fold_in(key_of[6], 1), SEQUENCE_TOKENS // (TOK_DEV // N_HEAD))
    route_ids_turns = jax.random.permutation(jax.random.fold_in(key_of[6], 3), SEQUENCE_TOKENS // (TOK_DEV // N_HEAD))
    route_ids = jax.vmap(lambda own, number: assign_block(jax.random.fold_in(key_of[6], 2), own, number, TOK_DEV // N_HEAD, EXPERTS, TOP, CAP, 2))(route_ids_keys, route_ids_turns).reshape((SEQUENCE_TOKENS, TOP))
    route_weights = jnp.clip(jnp.exp(math.log(1.0) - 2.9957323 * jax.random.uniform(key_of[7], (SEQUENCE_TOKENS, TOP), jnp.float32) ** block_scale(key_of[7], (SEQUENCE_TOKENS, TOP), ((0, 32),), -0.2, 0.2)), 0.05, 1.0)
    w_gate = scatter_about(key_of[8], (EXPERTS, D, HID), D ** -0.5, 0.109375, ((0, 8), (2, 4)))
    w_up = scatter_about(key_of[9], (EXPERTS, D, HID), D ** -0.5, 0.109375, ((0, 8), (2, 4)))
    w_down = scatter_about(key_of[10], (EXPERTS, HID, D), HID ** -0.5, 0.15625, ((0, 8), (1, 4)))
    return {"queries": queries, "keys": keys, "values": values, "residual": residual, "out_projection": out_projection, "norm_gain": norm_gain, "route_ids": route_ids, "route_weights": route_weights, "w_gate": w_gate, "w_up": w_up, "w_down": w_down}


EPSILON = 1e-05
SLOPE = 1.702

def attend_band(queries, concatenated_keys, concatenated_values, window, head_size, group, anchor_position):
    tokens = queries.shape[0]
    block = min(tokens, 512)
    count = tokens // block
    heads = queries.shape[1] // head_size
    kv_heads = heads // group
    scale = head_size ** (-0.5)

    def one_block(index):
        begin = index * block
        query_part = lax.dynamic_slice_in_dim(queries, begin, block, 0).reshape(block, kv_heads, group, head_size)
        key_part = lax.dynamic_slice_in_dim(concatenated_keys, begin, block + window, 0).reshape(block + window, kv_heads, head_size)
        value_part = lax.dynamic_slice_in_dim(concatenated_values, begin, block + window, 0).reshape(block + window, kv_heads, head_size)
        scores = jnp.einsum('qgjd,kgd->gjqk', query_part.astype(jnp.float32), key_part.astype(jnp.float32)) * scale
        query_pos = anchor_position + begin + jnp.arange(block, dtype=jnp.int32)
        key_pos = anchor_position - window + begin + jnp.arange(block + window, dtype=jnp.int32)
        distance = query_pos[:, None] - key_pos[None, :]
        allowed = (distance >= 0) & (distance < window) & (key_pos[None, :] >= 0)
        scores = jnp.where(allowed, scores, -jnp.inf)
        highest = lax.optimization_barrier(jnp.max(scores, axis=-1, keepdims=True))
        weights = jnp.exp(scores - highest)
        weights = (weights / lax.optimization_barrier(jnp.sum(weights, axis=-1, keepdims=True))).astype(jnp.bfloat16)
        result = jnp.einsum('gjqk,kgd->qgjd', weights.astype(jnp.float32), value_part.astype(jnp.float32))
        return result.astype(jnp.bfloat16).reshape(block, heads * head_size)
    outputs = lax.map(one_block, jnp.arange(count, dtype=jnp.int32))
    return outputs.reshape(tokens, heads * head_size)

def reference(queries, keys, values, residual, out_projection, norm_gain, route_ids, route_weights, w_gate, w_up, w_down):
    column_indices = KEY_VALUE_HEADS * HEAD_DIMENSION
    padding = jnp.zeros((BAND_WIDTH_KEYS, column_indices), jnp.bfloat16)
    concatenated_keys = jnp.concatenate([padding, keys], axis=0)
    concatenated_values = jnp.concatenate([padding, values], axis=0)
    attended_rows = attend_band(queries, concatenated_keys, concatenated_values, BAND_WIDTH_KEYS, HEAD_DIMENSION, QUERY_HEADS // KEY_VALUE_HEADS, 0)
    attn_out = jnp.dot(attended_rows, out_projection, preferred_element_type=jnp.float32)
    hidden_state = residual.astype(jnp.float32) + attn_out
    mean_square = lax.optimization_barrier(jnp.mean(hidden_state * hidden_state, axis=1, keepdims=True))
    normed = (hidden_state * lax.rsqrt(mean_square + EPSILON) * norm_gain.astype(jnp.float32)[None, :]).astype(jnp.bfloat16)
    flat_ids = route_ids.reshape(-1).astype(jnp.int32)
    flat_weights = route_weights.reshape(-1).astype(jnp.float32)
    total = flat_ids.shape[0]
    bound = min(total, SEQUENCE_TOKENS // (TOK_DEV // N_HEAD) * CAP)

    def run_expert(carry, expert):
        member = flat_ids == expert
        position = jnp.cumsum(member.astype(jnp.int32)) - 1
        target = jnp.where(member, position, bound).astype(jnp.int32)
        chosen = jnp.zeros((bound,), jnp.int32).at[target].set(jnp.arange(total, dtype=jnp.int32), mode='drop')
        valid = jnp.zeros((bound,), jnp.float32).at[target].set(1.0, mode='drop')
        token_rows = (chosen // TOP).astype(jnp.int32)
        inputs = normed[token_rows]
        gate = jnp.dot(inputs, w_gate[expert], preferred_element_type=jnp.float32)
        upward = jnp.dot(inputs, w_up[expert], preferred_element_type=jnp.float32)
        active = ((upward + 1.0) * gate * jax.nn.sigmoid(SLOPE * gate)).astype(jnp.bfloat16)
        expert_out = jnp.dot(active, w_down[expert], preferred_element_type=jnp.float32).astype(jnp.bfloat16)
        scaled = (flat_weights[chosen] * valid)[:, None] * expert_out.astype(jnp.float32)
        return (carry.at[token_rows].add(scaled), None)
    moe, _ = lax.scan(run_expert, jnp.zeros((SEQUENCE_TOKENS, D), jnp.float32), jnp.arange(EXPERTS, dtype=jnp.int32))
    return (hidden_state + moe).astype(jnp.bfloat16)
```

```python
import jax
import jax.numpy as jnp
from jax import lax
from jax.experimental import pallas as pl
from jax.experimental.pallas import tpu as pltpu
from jax.sharding import PartitionSpec as P

D = 2880
QUERY_HEADS = 32
KEY_VALUE_HEADS = 4
HEAD_DIMENSION = 64
BAND_WIDTH_KEYS = 128
TOP = 4


EPSILON = 1e-05
SLOPE = 1.702


def from_behind(x, axis, by):
    devices = lax.axis_size(axis)
    pairs = [(i, i + by) for i in range(devices) if 0 <= i + by < devices]
    return lax.ppermute(x, axis, pairs)


def attend_band(
    queries, concatenated_keys, concatenated_values, window, head_size, group, anchor_position
):
    tokens = queries.shape[0]
    block = min(tokens, 512)
    count = tokens // block
    heads = queries.shape[1] // head_size
    kv_heads = heads // group
    scale = head_size ** (-0.5)

    def one_block(index):
        begin = index * block
        query_part = queries.reshape(block, kv_heads, group, head_size)
        key_part = concatenated_keys.reshape(block + window, kv_heads, head_size)
        value_part = concatenated_values.reshape(block + window, kv_heads, head_size)
        scores = (
            jnp.einsum("qgjd,kgd->gjqk", query_part, key_part, preferred_element_type=jnp.float32)
            * scale
        )
        query_pos = anchor_position + begin + jnp.arange(block, dtype=jnp.int32)
        key_pos = anchor_position - window + begin + jnp.arange(block + window, dtype=jnp.int32)
        distance = query_pos[:, None] - key_pos[None, :]
        allowed = (distance >= 0) & (distance < window) & (key_pos[None, :] >= 0)
        scores = jnp.where(allowed, scores, -jnp.inf)
        highest = jnp.max(scores, axis=-1, keepdims=True)
        weights = jnp.exp(scores - highest)
        weights = (weights / jnp.sum(weights, axis=-1, keepdims=True)).astype(jnp.bfloat16)
        result = jnp.einsum(
            "gjqk,kgd->qgjd", weights, value_part, preferred_element_type=jnp.float32
        )
        return result.astype(jnp.bfloat16).reshape(block, heads * head_size)

    outputs = lax.map(one_block, jnp.arange(count, dtype=jnp.int32))
    return outputs.reshape(tokens, heads * head_size)


def expert_rows(inputs, gate_slice, up_slice, down_slice):
    gate = jnp.dot(inputs, gate_slice, preferred_element_type=jnp.float32)
    upward = jnp.dot(inputs, up_slice, preferred_element_type=jnp.float32)
    active = ((upward + 1.0) * gate * jax.nn.sigmoid(SLOPE * gate)).astype(jnp.bfloat16)
    return jnp.dot(active, down_slice, preferred_element_type=jnp.float32)


def sparse_plan(
    queries,
    keys,
    values,
    residual,
    out_projection,
    norm_gain,
    route_ids,
    route_weights,
    w_gate,
    w_up,
    w_down,
):
    tokens = queries.shape[0]
    key_band_extent = keys.shape[1]
    stacked = jnp.concatenate([keys, values], axis=1)
    prior = from_behind(stacked, ("ctx", "exp"), 1)
    joined_heads = jnp.concatenate([prior, stacked], axis=0)
    anchor_position = lax.axis_index(("ctx", "exp")) * tokens
    attended_rows = attend_band(
        queries,
        joined_heads[:, :key_band_extent],
        joined_heads[:, key_band_extent:],
        BAND_WIDTH_KEYS,
        HEAD_DIMENSION,
        QUERY_HEADS // KEY_VALUE_HEADS,
        anchor_position,
    )
    partial_sum = jnp.dot(
        attended_rows,
        lax.all_gather(out_projection, "exp", axis=1, tiled=True),
        preferred_element_type=jnp.float32,
    )
    attn_out = lax.psum_scatter(partial_sum, "head", scatter_dimension=0, tiled=True)
    hidden_state = residual.astype(jnp.float32) + attn_out
    mean_square = jnp.mean(hidden_state * hidden_state, axis=1, keepdims=True)
    normed = (hidden_state * lax.rsqrt(mean_square + EPSILON) * norm_gain[None, :]).astype(
        jnp.bfloat16
    )
    local_rows = normed.shape[0]
    experts = lax.axis_size("ctx") * lax.axis_size("head")
    capacity = max(2, TOP * tokens // experts)
    flat_ids = route_ids.reshape(-1)
    one_hot = (flat_ids[:, None] == jnp.arange(experts, dtype=jnp.int32)[None, :]).astype(jnp.int32)
    earlier = jnp.cumsum(one_hot, axis=0) - one_hot
    rank = jnp.sum(earlier * one_hot, axis=1)
    slot = flat_ids * capacity + rank
    outgoing = (
        jnp.zeros((experts * capacity, D), jnp.bfloat16)
        .at[slot]
        .set(jnp.repeat(normed, TOP, axis=0))
    )
    outgoing = outgoing.reshape(experts, capacity, D)
    arrived = lax.all_to_all(outgoing, ("ctx", "head"), split_axis=0, concat_axis=0, tiled=True)
    pooled = lax.all_gather(arrived, "exp", axis=0, tiled=True)
    partial_rows = expert_rows(
        pooled.reshape(experts * lax.axis_size("exp") * capacity, D), w_gate[0], w_up[0], w_down[0]
    )
    summed = lax.psum_scatter(
        partial_rows.reshape(experts * lax.axis_size("exp"), capacity, D),
        "exp",
        scatter_dimension=0,
        tiled=True,
    ).astype(jnp.bfloat16)
    returned = lax.all_to_all(summed, ("ctx", "head"), split_axis=0, concat_axis=0, tiled=True)
    flat_back = returned.reshape(experts * capacity, D)
    picked = flat_back[slot].astype(jnp.float32).reshape(local_rows, TOP, D)
    moe = jnp.sum(picked * route_weights[:, :, None], axis=1)
    return (hidden_state + moe).astype(jnp.bfloat16)


def swapped(x, axis, by):
    return lax.ppermute(x, axis, [(i, i ^ by) for i in range(lax.axis_size(axis))])


def fast_params(limit):
    return pltpu.CompilerParams(vmem_limit_bytes=limit)


VMEM = pl.BlockSpec(memory_space=pltpu.VMEM)
SMEM = pl.BlockSpec(memory_space=pltpu.SMEM)
ANY = pl.BlockSpec(memory_space=pl.ANY)


def attention_kernel(where_ref, q_ref, prior_ref, own_ref, mine_ref, other_ref, done_ref):
    tokens = q_ref.shape[0]
    width = own_ref.shape[1] // 2
    size = HEAD_DIMENSION
    group = QUERY_HEADS // KEY_VALUE_HEADS
    kv_heads = width // size
    pairs = group // 2
    scale = size ** (-0.5)
    row = lax.broadcasted_iota(jnp.int32, (tokens, 2 * tokens), 0)
    col = lax.broadcasted_iota(jnp.int32, (tokens, 2 * tokens), 1)
    distance = row + tokens - col
    allowed = (distance >= 0) & (distance < BAND_WIDTH_KEYS)
    allowed = allowed & (col + (where_ref[0] - tokens) >= 0)
    allowed = jnp.concatenate([allowed.astype(jnp.int32)] * pairs, axis=0) > 0
    lane = lax.broadcasted_iota(jnp.int32, (2 * tokens, 2 * size), 1)

    def halves(begin, g):
        tile = (g * size) // (2 * size) * (2 * size) + begin
        both = jnp.concatenate(
            [prior_ref[:, tile : tile + 2 * size], own_ref[:, tile : tile + 2 * size]], axis=0
        ).astype(jnp.float32)
        turned = pltpu.roll(both, size, 1)
        low, high = (both, turned) if g % 2 == 0 else (turned, both)
        low = jnp.where(lane < size, low, 0.0).astype(jnp.bfloat16)
        high = jnp.where(lane >= size, high, 0.0).astype(jnp.bfloat16)
        return low, high

    def weights_of(stacked, k):
        s = lax.dot_general(
            stacked, k, (((1,), (1,)), ((), ())), preferred_element_type=jnp.float32
        )
        s = jnp.where(allowed, s * scale, -jnp.inf)
        w = jnp.exp(s - jnp.max(s, axis=-1, keepdims=True))
        return (w / jnp.sum(w, axis=-1, keepdims=True)).astype(jnp.bfloat16)

    for g in range(kv_heads):
        k_low, k_high = halves(0, g)
        v_low, v_high = halves(width, g)
        first = g * group * size
        stacked = jnp.concatenate(
            [q_ref[:, first + 2 * size * p : first + 2 * size * (p + 1)] for p in range(pairs)],
            axis=0,
        )
        result = jnp.dot(
            weights_of(stacked, k_low), v_low, preferred_element_type=jnp.float32
        ) + jnp.dot(weights_of(stacked, k_high), v_high, preferred_element_type=jnp.float32)
        result = result.astype(jnp.bfloat16)
        for p in range(pairs):
            done_ref[:, first + 2 * size * p : first + 2 * size * (p + 1)] = result[
                p * tokens : (p + 1) * tokens
            ]
    half = tokens // 2
    head = where_ref[1]
    mine_ref[...] = done_ref[pl.ds(pl.multiple_of(head * half, half), half), :]
    other_ref[...] = done_ref[pl.ds(pl.multiple_of((1 - head) * half, half), half), :]


def attention(where, queries, prior, own):
    tokens, width = queries.shape
    half = jax.ShapeDtypeStruct((tokens // 2, width), jnp.bfloat16)
    return pl.pallas_call(
        attention_kernel,
        out_shape=(half, half),
        in_specs=[SMEM, VMEM, VMEM, VMEM],
        out_specs=(VMEM, VMEM),
        scratch_shapes=[pltpu.VMEM((tokens, width), jnp.bfloat16)],
        compiler_params=fast_params(32 << 20),
        cost_estimate=pl.CostEstimate(
            flops=8 * tokens * tokens * width, bytes_accessed=4 * tokens * width, transcendentals=0
        ),
        name="attention",
    )(where, queries, prior, own)


def project_kernel(
    columns, where_ref, a0, a1, a2, a3, r0, r1, r2, r3, w_ref, wp_ref, gain_ref,
    block_ref, attn_ref, a_all, r_all,
):
    me = where_ref[0]
    rows, half = a0.shape
    half = half // 2
    for s, (a, r) in enumerate(((a0, r0), (a1, r1), (a2, r2), (a3, r3))):
        at = pl.ds(pl.multiple_of((me ^ s) * rows, rows), rows)
        a_all[at, :] = a[...]
        r_all[at, :] = r[...]
    attn = jnp.dot(a_all[:, :half], w_ref[...], preferred_element_type=jnp.float32)
    attn += jnp.dot(a_all[:, half:], wp_ref[...], preferred_element_type=jnp.float32)
    attn_ref[...] = attn.astype(jnp.bfloat16)
    hidden = r_all[...].astype(jnp.float32) + attn
    lane = lax.broadcasted_iota(jnp.int32, hidden.shape, 1)
    square = jnp.sum(jnp.where(lane < columns, hidden * hidden, 0.0), axis=1, keepdims=True)
    high = square.astype(jnp.bfloat16).astype(jnp.float32)
    block = hidden * gain_ref[...]
    block = jnp.where(lane == columns, high, block)
    block = jnp.where(lane == columns + 1, square - high, block)
    block_ref[...] = block.astype(jnp.bfloat16)


def project(me, blocks, rests, w_own, w_partner, gain, columns):
    rows, width = blocks[0].shape
    padded = w_own.shape[1]
    out = jax.ShapeDtypeStruct((4 * rows, padded), jnp.bfloat16)
    return pl.pallas_call(
        lambda *refs: project_kernel(columns, *refs),
        out_shape=(out, out),
        in_specs=[SMEM] + [VMEM] * 11,
        out_specs=(VMEM, VMEM),
        scratch_shapes=[
            pltpu.VMEM((4 * rows, width), jnp.bfloat16),
            pltpu.VMEM((4 * rows, padded), jnp.bfloat16),
        ],
        compiler_params=fast_params(32 << 20),
        cost_estimate=pl.CostEstimate(
            flops=8 * rows * width * padded, bytes_accessed=4 * width * padded, transcendentals=0
        ),
        name="project",
    )(me, *blocks, *rests, w_own, w_partner, gain)


def experts_kernel(
    columns, experts, with_attn, where_ref, x0, x1, x2, x3a, x3b, *refs
):
    placed_ref = refs[0] if with_attn else None
    refs = refs[1:] if with_attn else refs
    weights, refs = refs[:6], refs[6:]
    own_ref, keep_ref, sx_ref, sy_ref, wg, wu, wd, act_ref, sems = refs
    me = where_ref[0]
    hid = weights[0].shape[1]
    copies = []
    for s in range(4):
        at = pl.ds(pl.multiple_of((me ^ s) * columns, 16), columns)
        group = []
        for j in range(2):
            for k, to in ((0, wg), (1, wu)):
                group.append(
                    pltpu.make_async_copy(
                        weights[3 * j + k].at[at, :],
                        to.at[s, pl.ds(0, columns), pl.ds(j * hid, hid)],
                        sems.at[4 * s + 2 * j + k],
                    )
                )
        copies.append(group)
    down = [
        pltpu.make_async_copy(
            weights[3 * j + 2], wd.at[pl.ds(j * hid, hid), :], sems.at[16 + j]
        )
        for j in range(2)
    ]
    for group in copies:
        for copy in group:
            copy.start()
    for copy in down:
        copy.start()
    padded = x0.shape[1]
    rows = x0.shape[0]
    rest = padded - columns
    for s in range(4):
        wg[s, columns:, :] = jnp.zeros((rest, 2 * hid), jnp.bfloat16)
        wu[s, columns:, :] = jnp.zeros((rest, 2 * hid), jnp.bfloat16)
    tail = columns // 128 * 128
    lane = lax.broadcasted_iota(jnp.int32, (rows, padded - tail), 1) + tail

    def column(x, *at):
        hit = lane == at[0]
        for other in at[1:]:
            hit = hit | (lane == other)
        return jnp.sum(jnp.where(hit, x, 0.0), axis=1, keepdims=True)

    tails = [
        x0[:, tail:].astype(jnp.float32),
        x1[:, tail:].astype(jnp.float32),
        x2[:, tail:].astype(jnp.float32),
        jnp.concatenate([x3a[:, tail:], x3b[:, tail:]], axis=0).astype(jnp.float32),
    ]
    square = column(tails[0] + tails[1] + tails[2] + tails[3], columns, columns + 1)
    r = lax.rsqrt(square * (1.0 / (4 * columns)) + EPSILON)
    base = columns + 2
    share = [
        column(tails[0], base + where_ref[1 + j], base + experts + where_ref[1 + j])
        for j in range(2)
    ]
    gate = upward = None
    for s in range(4):
        for copy in copies[s]:
            copy.wait()
        x = (x0, x1, x2)[s][...] if s < 3 else jnp.concatenate([x3a[...], x3b[...]], axis=0)
        g = jnp.dot(x, wg[s], preferred_element_type=jnp.float32)
        u = jnp.dot(x, wu[s], preferred_element_type=jnp.float32)
        gate = g if gate is None else gate + g
        upward = u if upward is None else upward + u
    gate = gate * r
    upward = upward * r
    active = (upward + 1.0) * gate * jax.nn.sigmoid(SLOPE * gate)
    for j in range(2):
        at = slice(j * hid, (j + 1) * hid)
        act_ref[:, at] = (active[:, at] * share[j]).astype(jnp.bfloat16)
    for copy in down:
        copy.wait()
    piece = rows // 4
    part = piece // 2
    order = ((0, 0), (0, 1), (1, 0), (3, 0), (2, 1), (3, 1), (2, 0), (1, 1))

    def ordered(ref):
        return jnp.concatenate(
            [
                ref[pl.ds(pl.multiple_of((me ^ s) * piece + b * part, part), part), :]
                for s, b in order
            ],
            axis=0,
        )

    act = ordered(act_ref)
    total = wd.shape[1]
    step = 768
    for begin in range(0, total, step):
        end = min(total, begin + step)
        out = jnp.dot(act, wd[:, begin:end], preferred_element_type=jnp.float32)
        if with_attn:
            out += jnp.concatenate(
                [
                    placed_ref[
                        pl.ds(pl.multiple_of((me ^ s) * piece + b * part, part), part), begin:end
                    ]
                    for s, b in order
                ],
                axis=0,
            ).astype(jnp.float32)
        own_ref[:, begin:end] = out[:piece]
        sx_ref[:, begin:end] = out[piece : 2 * piece].astype(jnp.bfloat16)
        sy_ref[:, begin:end] = out[2 * piece : 3 * piece].astype(jnp.bfloat16)
        keep_ref[:, begin:end] = out[3 * piece :]


def expert_chunk(where, blocks, weights, placed, columns, experts):
    rows, padded = blocks[0].shape
    hid, total = weights[2].shape
    piece = rows // 4
    extra = () if placed is None else (placed,)
    f32 = jax.ShapeDtypeStruct((piece, total), jnp.float32)
    b16 = jax.ShapeDtypeStruct((piece, total), jnp.bfloat16)
    return pl.pallas_call(
        lambda *refs: experts_kernel(columns, experts, placed is not None, *refs),
        out_shape=(f32, f32, b16, b16),
        in_specs=[SMEM] + [VMEM] * (5 + len(extra)) + [ANY] * 6,
        out_specs=(VMEM,) * 4,
        scratch_shapes=[
            pltpu.VMEM((4, padded, 2 * hid), jnp.bfloat16),
            pltpu.VMEM((4, padded, 2 * hid), jnp.bfloat16),
            pltpu.VMEM((2 * hid, total), jnp.bfloat16),
            pltpu.VMEM((rows, 2 * hid), jnp.bfloat16),
            pltpu.SemaphoreType.DMA((18,)),
        ],
        compiler_params=fast_params(44 << 20),
        cost_estimate=pl.CostEstimate(
            flops=12 * rows * hid * total, bytes_accessed=12 * hid * total, transcendentals=0
        ),
        name="experts",
    )(where, *blocks, *extra, *weights)


def gather_plane(block):
    half = block.shape[0] // 2
    beside = swapped(block, "exp", 1)
    across = swapped(block, "exp", 2)
    far_a = swapped(across[:half], "exp", 1)
    far_b = swapped(beside[half:], "exp", 2)
    return block, beside, across, far_a, far_b


def reduce_plane(own, keep, sx, sy):
    part = own.shape[0] // 2
    gx = swapped(sx, "exp", 1).astype(jnp.float32)
    gy = swapped(sy, "exp", 2).astype(jnp.float32)
    onward_y = (keep[:part] + gx[part:]).astype(jnp.bfloat16)
    onward_x = (keep[part:] + gy[part:]).astype(jnp.bfloat16)
    fy = swapped(onward_y, "exp", 2).astype(jnp.float32)
    fx = swapped(onward_x, "exp", 1).astype(jnp.float32)
    return own + jnp.concatenate([gx[:part] + fy, gy[:part] + fx], axis=0)


def dense_plan(
    queries,
    keys,
    values,
    residual,
    out_projection,
    norm_gain,
    route_ids,
    route_weights,
    w_gate,
    w_up,
    w_down,
):
    tokens = queries.shape[0]
    rows, total = residual.shape
    columns = out_projection.shape[1]
    spare = -columns % 128
    experts = lax.axis_size("ctx") * lax.axis_size("head")
    z, e, h = lax.axis_index("ctx"), lax.axis_index("exp"), lax.axis_index("head")
    i32 = jnp.int32

    own = jnp.concatenate([keys, values], axis=1)
    prior = from_behind(own, ("ctx", "exp"), 1)

    chosen = route_ids[:, :, None] == jnp.arange(experts, dtype=i32)[None, None, :]
    shares = jnp.sum(jnp.where(chosen, route_weights[:, :, None], 0.0), axis=1)
    high = lax.reduce_precision(shares, 8, 7)
    notes = jnp.concatenate([jnp.zeros((rows, 2), jnp.float32), high, shares - high], axis=1)
    notes = jnp.pad(notes, ((0, 0), (0, spare - notes.shape[1]))).astype(jnp.bfloat16)
    packed = jnp.stack(
        [
            jnp.concatenate([residual[:, columns * k : columns * (k + 1)], notes], axis=1)
            for k in range(4)
        ]
    )
    rests = [lax.dynamic_index_in_dim(packed, e ^ s, 0, keepdims=False) for s in range(4)]
    rests = [rests[0]] + [swapped(rests[s], "exp", s) for s in range(1, 4)]
    w_own = jnp.pad(out_projection, ((0, 0), (0, spare)))
    w_partner = swapped(w_own, "head", 1)
    gain = lax.dynamic_slice_in_dim(norm_gain, e * columns, columns, 0)
    gain = jnp.pad(gain, (0, spare), constant_values=1.0)[None, :]
    mats = [w_gate[0], w_up[0], w_down[0]]
    weights = mats + [swapped(m, "head", 1) for m in mats]

    place = jnp.stack([(z * 4 + e) * tokens, h]).astype(i32)
    mine, other = attention(place, queries, prior, own)
    theirs = swapped(other, "head", 1)
    both = jnp.concatenate([mine, theirs], axis=1)
    blocks = [both] + [swapped(both, "exp", s) for s in range(1, 4)]
    block, attn = project(e[None].astype(i32), blocks, rests, w_own, w_partner, gain, columns)
    placed = jnp.concatenate(
        [jnp.where(e == k, attn[:, :columns], jnp.bfloat16(0)) for k in range(4)], axis=1
    )

    where = jnp.stack([e, z * 2 + h, z * 2 + 1 - h]).astype(i32)
    planes = lax.axis_size("ctx")
    arrived = [block] + [swapped(block, "ctx", s) for s in range(1, planes)]
    sums = [None] * planes
    for s in [*range(1, planes), 0]:
        gathered = gather_plane(arrived[s])
        parts = expert_chunk(
            where, gathered, weights, placed if s == 0 else None, columns, experts
        )
        sums[s] = reduce_plane(*parts)
    mixed = residual.astype(jnp.float32) + sums[0]
    for s in range(1, planes):
        back = swapped(sums[s].astype(jnp.bfloat16), "ctx", s)
        mixed = mixed + back.astype(jnp.float32)
    return mixed.astype(jnp.bfloat16)


def local(*arrays):
    queries, out_projection, residual = arrays[0], arrays[4], arrays[3]
    tokens = queries.shape[0]
    planes, heads = lax.axis_size("ctx"), lax.axis_size("head")
    experts = planes * heads
    rows = residual.shape[0]
    spare = -out_projection.shape[1] % 128
    dense = (
        max(2, TOP * tokens // experts) >= rows
        and heads == 2
        and lax.axis_size("exp") == 4
        and planes & (planes - 1) == 0
        and tokens == BAND_WIDTH_KEYS
        and 2 + 2 * experts <= spare
    )
    return (dense_plan if dense else sparse_plan)(*arrays)


def solution(mesh):
    return jax.shard_map(
        local,
        mesh=mesh,
        in_specs=(
            P(("ctx", "exp"), "head"),
            P(("ctx", "exp"), "head"),
            P(("ctx", "exp"), "head"),
            P(("ctx", "exp", "head"), None),
            P("head", "exp"),
            P(),
            P(("ctx", "exp", "head"), None),
            P(("ctx", "exp", "head"), None),
            P(("ctx", "head"), None, "exp"),
            P(("ctx", "head"), None, "exp"),
            P(("ctx", "head"), "exp", None),
        ),
        out_specs=P(("ctx", "exp", "head"), None),
        check_vma=False,
    )
```

```python
import jax
import jax.numpy as jnp
from jax import lax
from jax.experimental import pallas as pl
from jax.experimental.pallas import tpu as pltpu
from jax.sharding import PartitionSpec as P

D = 2880
QUERY_HEADS = 32
KEY_VALUE_HEADS = 4
HEAD_DIMENSION = 64
BAND_WIDTH_KEYS = 128
TOP = 4


EPSILON = 1e-05
SLOPE = 1.702


def from_behind(x, axis, by):
    devices = lax.axis_size(axis)
    pairs = [(i, i + by) for i in range(devices) if 0 <= i + by < devices]
    return lax.ppermute(x, axis, pairs)


def attend_band(
    queries, concatenated_keys, concatenated_values, window, head_size, group, anchor_position
):
    tokens = queries.shape[0]
    block = min(tokens, 512)
    count = tokens // block
    heads = queries.shape[1] // head_size
    kv_heads = heads // group
    scale = head_size ** (-0.5)

    def one_block(index):
        begin = index * block
        query_part = queries.reshape(block, kv_heads, group, head_size)
        key_part = concatenated_keys.reshape(block + window, kv_heads, head_size)
        value_part = concatenated_values.reshape(block + window, kv_heads, head_size)
        scores = (
            jnp.einsum("qgjd,kgd->gjqk", query_part, key_part, preferred_element_type=jnp.float32)
            * scale
        )
        query_pos = anchor_position + begin + jnp.arange(block, dtype=jnp.int32)
        key_pos = anchor_position - window + begin + jnp.arange(block + window, dtype=jnp.int32)
        distance = query_pos[:, None] - key_pos[None, :]
        allowed = (distance >= 0) & (distance < window) & (key_pos[None, :] >= 0)
        scores = jnp.where(allowed, scores, -jnp.inf)
        highest = jnp.max(scores, axis=-1, keepdims=True)
        weights = jnp.exp(scores - highest)
        weights = (weights / jnp.sum(weights, axis=-1, keepdims=True)).astype(jnp.bfloat16)
        result = jnp.einsum(
            "gjqk,kgd->qgjd", weights, value_part, preferred_element_type=jnp.float32
        )
        return result.astype(jnp.bfloat16).reshape(block, heads * head_size)

    outputs = lax.map(one_block, jnp.arange(count, dtype=jnp.int32))
    return outputs.reshape(tokens, heads * head_size)


def expert_rows(inputs, gate_slice, up_slice, down_slice):
    gate = jnp.dot(inputs, gate_slice, preferred_element_type=jnp.float32)
    upward = jnp.dot(inputs, up_slice, preferred_element_type=jnp.float32)
    active = ((upward + 1.0) * gate * jax.nn.sigmoid(SLOPE * gate)).astype(jnp.bfloat16)
    return jnp.dot(active, down_slice, preferred_element_type=jnp.float32)


def sparse_plan(
    queries,
    keys,
    values,
    residual,
    out_projection,
    norm_gain,
    route_ids,
    route_weights,
    w_gate,
    w_up,
    w_down,
):
    tokens = queries.shape[0]
    key_band_extent = keys.shape[1]
    stacked = jnp.concatenate([keys, values], axis=1)
    prior = from_behind(stacked, ("ctx", "exp"), 1)
    joined_heads = jnp.concatenate([prior, stacked], axis=0)
    anchor_position = lax.axis_index(("ctx", "exp")) * tokens
    attended_rows = attend_band(
        queries,
        joined_heads[:, :key_band_extent],
        joined_heads[:, key_band_extent:],
        BAND_WIDTH_KEYS,
        HEAD_DIMENSION,
        QUERY_HEADS // KEY_VALUE_HEADS,
        anchor_position,
    )
    partial_sum = jnp.dot(
        attended_rows,
        lax.all_gather(out_projection, "exp", axis=1, tiled=True),
        preferred_element_type=jnp.float32,
    )
    attn_out = lax.psum_scatter(partial_sum, "head", scatter_dimension=0, tiled=True)
    hidden_state = residual.astype(jnp.float32) + attn_out
    mean_square = jnp.mean(hidden_state * hidden_state, axis=1, keepdims=True)
    normed = (hidden_state * lax.rsqrt(mean_square + EPSILON) * norm_gain[None, :]).astype(
        jnp.bfloat16
    )
    local_rows = normed.shape[0]
    experts = lax.axis_size("ctx") * lax.axis_size("head")
    capacity = max(2, TOP * tokens // experts)
    flat_ids = route_ids.reshape(-1)
    one_hot = (flat_ids[:, None] == jnp.arange(experts, dtype=jnp.int32)[None, :]).astype(jnp.int32)
    earlier = jnp.cumsum(one_hot, axis=0) - one_hot
    rank = jnp.sum(earlier * one_hot, axis=1)
    slot = flat_ids * capacity + rank
    outgoing = (
        jnp.zeros((experts * capacity, D), jnp.bfloat16)
        .at[slot]
        .set(jnp.repeat(normed, TOP, axis=0))
    )
    outgoing = outgoing.reshape(experts, capacity, D)
    arrived = lax.all_to_all(outgoing, ("ctx", "head"), split_axis=0, concat_axis=0, tiled=True)
    pooled = lax.all_gather(arrived, "exp", axis=0, tiled=True)
    partial_rows = expert_rows(
        pooled.reshape(experts * lax.axis_size("exp") * capacity, D), w_gate[0], w_up[0], w_down[0]
    )
    summed = lax.psum_scatter(
        partial_rows.reshape(experts * lax.axis_size("exp"), capacity, D),
        "exp",
        scatter_dimension=0,
        tiled=True,
    ).astype(jnp.bfloat16)
    returned = lax.all_to_all(summed, ("ctx", "head"), split_axis=0, concat_axis=0, tiled=True)
    flat_back = returned.reshape(experts * capacity, D)
    picked = flat_back[slot].astype(jnp.float32).reshape(local_rows, TOP, D)
    moe = jnp.sum(picked * route_weights[:, :, None], axis=1)
    return (hidden_state + moe).astype(jnp.bfloat16)


def swapped(x, axis, by):
    return lax.ppermute(x, axis, [(i, i ^ by) for i in range(lax.axis_size(axis))])


def fast_params(limit):
    return pltpu.CompilerParams(vmem_limit_bytes=limit)


VMEM = pl.BlockSpec(memory_space=pltpu.VMEM)
SMEM = pl.BlockSpec(memory_space=pltpu.SMEM)
ANY = pl.BlockSpec(memory_space=pl.ANY)


def attention_kernel(
    where_ref, q_ref, prior_k, own_k, prior_v, own_v, mine_ref, other_ref, done_ref
):
    tokens = q_ref.shape[0]
    width = own_k.shape[1]
    size = HEAD_DIMENSION
    group = QUERY_HEADS // KEY_VALUE_HEADS
    kv_heads = width // size
    pairs = group // 2
    scale = size ** (-0.5)
    row = lax.broadcasted_iota(jnp.int32, (tokens, 2 * tokens), 0)
    col = lax.broadcasted_iota(jnp.int32, (tokens, 2 * tokens), 1)
    distance = row + tokens - col
    allowed = (distance >= 0) & (distance < BAND_WIDTH_KEYS)
    allowed = allowed & (col + (where_ref[0] - tokens) >= 0)
    allowed = jnp.concatenate([allowed.astype(jnp.int32)] * pairs, axis=0) > 0
    lane = lax.broadcasted_iota(jnp.int32, (2 * tokens, 2 * size), 1)

    def halves(prior, own, g):
        tile = (g * size) // (2 * size) * (2 * size)
        both = jnp.concatenate(
            [prior[:, tile : tile + 2 * size], own[:, tile : tile + 2 * size]], axis=0
        ).astype(jnp.float32)
        turned = pltpu.roll(both, size, 1)
        low, high = (both, turned) if g % 2 == 0 else (turned, both)
        low = jnp.where(lane < size, low, 0.0).astype(jnp.bfloat16)
        high = jnp.where(lane >= size, high, 0.0).astype(jnp.bfloat16)
        return low, high

    def weights_of(stacked, k):
        s = lax.dot_general(
            stacked, k, (((1,), (1,)), ((), ())), preferred_element_type=jnp.float32
        )
        s = jnp.where(allowed, s * scale, -jnp.inf)
        w = jnp.exp(s - jnp.max(s, axis=-1, keepdims=True))
        return (w / jnp.sum(w, axis=-1, keepdims=True)).astype(jnp.bfloat16)

    for g in range(kv_heads):
        k_low, k_high = halves(prior_k, own_k, g)
        v_low, v_high = halves(prior_v, own_v, g)
        first = g * group * size
        stacked = jnp.concatenate(
            [q_ref[:, first + 2 * size * p : first + 2 * size * (p + 1)] for p in range(pairs)],
            axis=0,
        )
        result = jnp.dot(
            weights_of(stacked, k_low), v_low, preferred_element_type=jnp.float32
        ) + jnp.dot(weights_of(stacked, k_high), v_high, preferred_element_type=jnp.float32)
        result = result.astype(jnp.bfloat16)
        for p in range(pairs):
            done_ref[:, first + 2 * size * p : first + 2 * size * (p + 1)] = result[
                p * tokens : (p + 1) * tokens
            ]
    half = tokens // 2
    head = where_ref[1]
    mine_ref[...] = done_ref[pl.ds(pl.multiple_of(head * half, half), half), :]
    other_ref[...] = done_ref[pl.ds(pl.multiple_of((1 - head) * half, half), half), :]


def attention(where, queries, *bands):
    tokens, width = queries.shape
    half = jax.ShapeDtypeStruct((tokens // 2, width), jnp.bfloat16)
    return pl.pallas_call(
        attention_kernel,
        out_shape=(half, half),
        in_specs=[SMEM] + [VMEM] * 5,
        out_specs=(VMEM, VMEM),
        scratch_shapes=[pltpu.VMEM((tokens, width), jnp.bfloat16)],
        compiler_params=fast_params(32 << 20),
        cost_estimate=pl.CostEstimate(
            flops=8 * tokens * tokens * width, bytes_accessed=4 * tokens * width, transcendentals=0
        ),
        name="attention",
    )(where, queries, *bands)


def pack_kernel(columns, experts, me_ref, rest_ref, ids_ref, share_ref, *refs):
    outs, packed, notes = refs[:4], refs[4], refs[5]
    me = me_ref[0]
    rows, padded = outs[0].shape
    spare = padded - columns
    lane = lax.broadcasted_iota(jnp.int32, (rows, spare), 1)
    high = jnp.zeros((rows, spare), jnp.float32)
    low = jnp.zeros((rows, spare), jnp.float32)
    for k in range(ids_ref.shape[1]):
        at = ids_ref[:, k : k + 1] + 2
        value = share_ref[:, k : k + 1]
        top = value.astype(jnp.bfloat16).astype(jnp.float32)
        high += jnp.where(lane == at, top, 0.0)
        low += jnp.where(lane == at + experts, value - top, 0.0)
    notes[...] = high + low
    for k in range(4):
        packed[k, :, :columns] = rest_ref[:, k * columns : (k + 1) * columns]
        packed[k, :, columns:] = notes[...].astype(jnp.bfloat16)
    for s in range(4):
        outs[s][...] = packed[me ^ s]


def pack(me, residual, ids, shares, columns, padded, experts):
    rows = residual.shape[0]
    out = jax.ShapeDtypeStruct((rows, padded), jnp.bfloat16)
    return pl.pallas_call(
        lambda *refs: pack_kernel(columns, experts, *refs),
        out_shape=(out,) * 4,
        in_specs=[SMEM] + [VMEM] * 3,
        out_specs=(VMEM,) * 4,
        scratch_shapes=[
            pltpu.VMEM((4, rows, padded), jnp.bfloat16),
            pltpu.VMEM((rows, padded - columns), jnp.float32),
        ],
        compiler_params=fast_params(16 << 20),
        cost_estimate=pl.CostEstimate(
            flops=rows * padded, bytes_accessed=16 * rows * padded, transcendentals=0
        ),
        name="pack",
    )(me, residual, ids, shares)


def project_kernel(columns, where_ref, *refs):
    mine, theirs, rests = refs[:4], refs[4:8], refs[8:12]
    w_ref, wp_ref, gain_ref, block_ref, attn_ref, a_all, r_all = refs[12:]
    me = where_ref[0]
    rows, half = mine[0].shape
    for s in range(4):
        at = pl.ds(pl.multiple_of((me ^ s) * rows, rows), rows)
        a_all[at, :half] = mine[s][...]
        a_all[at, half:] = theirs[s][...]
        r_all[at, :] = rests[s][...]
    across = (((1,), (1,)), ((), ()))
    attn = lax.dot_general(
        a_all[:, :half], w_ref[...], across, preferred_element_type=jnp.float32
    )
    attn += lax.dot_general(
        a_all[:, half:], wp_ref[...], across, preferred_element_type=jnp.float32
    )
    attn_ref[:, columns:] = jnp.zeros((4 * rows, attn_ref.shape[1] - columns), jnp.float32)
    attn_ref[:, :columns] = attn
    hidden = r_all[...].astype(jnp.float32) + attn_ref[...]
    lane = lax.broadcasted_iota(jnp.int32, hidden.shape, 1)
    square = jnp.sum(jnp.where(lane < columns, hidden * hidden, 0.0), axis=1, keepdims=True)
    high = square.astype(jnp.bfloat16).astype(jnp.float32)
    block = hidden * gain_ref[...]
    block = jnp.where(lane == columns, high, block)
    block = jnp.where(lane == columns + 1, square - high, block)
    block_ref[...] = block.astype(jnp.bfloat16)


def project(me, mine, theirs, rests, w_own, w_partner, gain):
    rows, half = mine[0].shape
    columns, padded = w_own.shape[0], gain.shape[1]
    return pl.pallas_call(
        lambda *refs: project_kernel(columns, *refs),
        out_shape=(
            jax.ShapeDtypeStruct((4 * rows, padded), jnp.bfloat16),
            jax.ShapeDtypeStruct((4 * rows, padded), jnp.float32),
        ),
        in_specs=[SMEM] + [VMEM] * 15,
        out_specs=(VMEM, VMEM),
        scratch_shapes=[
            pltpu.VMEM((4 * rows, 2 * half), jnp.bfloat16),
            pltpu.VMEM((4 * rows, padded), jnp.bfloat16),
        ],
        compiler_params=fast_params(32 << 20),
        cost_estimate=pl.CostEstimate(
            flops=16 * rows * half * padded, bytes_accessed=8 * half * padded, transcendentals=0
        ),
        name="project",
    )(me, *mine, *theirs, *rests, w_own, w_partner, gain)


def experts_kernel(
    columns, experts, with_attn, where_ref, x0, x1, x2, x3, *refs
):
    attn_ref, sum_ref = (refs[0], refs[-1]) if with_attn else (None, None)
    refs = refs[1:-1] if with_attn else refs
    weights, refs = refs[:6], refs[6:]
    own_ref, keep_ref, sx_ref, sy_ref, wg, wu, wd, act_ref, sems = refs
    me = where_ref[0]
    hid = weights[0].shape[1]
    copies = []
    for s in range(4):
        at = pl.ds(pl.multiple_of((me ^ s) * columns, 16), columns)
        group = []
        for j in range(2):
            for k, to in ((0, wg), (1, wu)):
                group.append(
                    pltpu.make_async_copy(
                        weights[3 * j + k].at[at, :],
                        to.at[s, pl.ds(0, columns), pl.ds(j * hid, hid)],
                        sems.at[4 * s + 2 * j + k],
                    )
                )
        copies.append(group)
    down = [
        pltpu.make_async_copy(
            weights[3 * j + 2], wd.at[:, pl.ds(j * hid, hid)], sems.at[16 + j]
        )
        for j in range(2)
    ]
    for group in copies:
        for copy in group:
            copy.start()
    for copy in down:
        copy.start()
    padded = x0.shape[1]
    rows = x0.shape[0]
    rest = padded - columns
    for s in range(4):
        wg[s, columns:, :] = jnp.zeros((rest, 2 * hid), jnp.bfloat16)
        wu[s, columns:, :] = jnp.zeros((rest, 2 * hid), jnp.bfloat16)
    tail = columns // 128 * 128
    lane = lax.broadcasted_iota(jnp.int32, (rows, padded - tail), 1) + tail

    def column(x, *at):
        hit = lane == at[0]
        for other in at[1:]:
            hit = hit | (lane == other)
        return jnp.sum(jnp.where(hit, x, 0.0), axis=1, keepdims=True)

    tails = [
        x0[:, tail:].astype(jnp.float32),
        x1[:, tail:].astype(jnp.float32),
        x2[:, tail:].astype(jnp.float32),
        x3[:, tail:].astype(jnp.float32),
    ]
    square = column(tails[0] + tails[1] + tails[2] + tails[3], columns, columns + 1)
    r = lax.rsqrt(square * (1.0 / (4 * columns)) + EPSILON)
    base = columns + 2
    share = [
        column(tails[0], base + where_ref[1 + j], base + experts + where_ref[1 + j])
        for j in range(2)
    ]
    gate = upward = None
    for s in range(4):
        for copy in copies[s]:
            copy.wait()
        x = (x0, x1, x2, x3)[s][...]
        g = jnp.dot(x, wg[s], preferred_element_type=jnp.float32)
        u = jnp.dot(x, wu[s], preferred_element_type=jnp.float32)
        gate = g if gate is None else gate + g
        upward = u if upward is None else upward + u
    gate = gate * r
    upward = upward * r
    active = (upward + 1.0) * gate * jax.nn.sigmoid(SLOPE * gate)
    for j in range(2):
        at = slice(j * hid, (j + 1) * hid)
        act_ref[:, at] = (active[:, at] * share[j]).astype(jnp.bfloat16)
    for copy in down:
        copy.wait()
    piece = rows // 4
    part = piece // 2
    order = ((0, 0), (0, 1), (1, 0), (3, 0), (2, 1), (3, 1), (2, 0), (1, 1))

    def ordered(ref):
        return jnp.concatenate(
            [
                ref[pl.ds(pl.multiple_of((me ^ s) * piece + b * part, part), part), :]
                for s, b in order
            ],
            axis=0,
        )

    act = ordered(act_ref)
    total = wd.shape[0]
    step = 768

    def put(at, out):
        own_ref[:, at] = out[:piece]
        sx_ref[:, at] = out[piece : 2 * piece].astype(jnp.bfloat16)
        sy_ref[:, at] = out[2 * piece : 3 * piece].astype(jnp.bfloat16)
        keep_ref[:, at] = out[3 * piece :]

    for begin in range(0, total, step):
        at = slice(begin, min(total, begin + step))
        out = lax.dot_general(
            act, wd[at, :], (((1,), (1,)), ((), ())), preferred_element_type=jnp.float32
        )
        if with_attn:
            sum_ref[:, at] = out
        else:
            put(at, out)
    if with_attn:
        attn = ordered(attn_ref)[:, :columns]
        for k in range(4):

            @pl.when(me == k)
            def _(k=k):
                sum_ref[:, k * columns : (k + 1) * columns] += attn

        put(slice(None), sum_ref[...])


def expert_chunk(where, blocks, weights, attn, columns, experts):
    rows, padded = blocks[0].shape
    total, hid = weights[2].shape
    piece = rows // 4
    extra = () if attn is None else (attn,)
    scratch = [] if attn is None else [pltpu.VMEM((rows, total), jnp.float32)]
    f32 = jax.ShapeDtypeStruct((piece, total), jnp.float32)
    b16 = jax.ShapeDtypeStruct((piece, total), jnp.bfloat16)
    return pl.pallas_call(
        lambda *refs: experts_kernel(columns, experts, attn is not None, *refs),
        out_shape=(f32, f32, b16, b16),
        in_specs=[SMEM] + [VMEM] * (4 + len(extra)) + [ANY] * 6,
        out_specs=(VMEM,) * 4,
        scratch_shapes=[
            pltpu.VMEM((4, padded, 2 * hid), jnp.bfloat16),
            pltpu.VMEM((4, padded, 2 * hid), jnp.bfloat16),
            pltpu.VMEM((total, 2 * hid), jnp.bfloat16),
            pltpu.VMEM((rows, 2 * hid), jnp.bfloat16),
            pltpu.SemaphoreType.DMA((18,)),
            *scratch,
        ],
        compiler_params=fast_params(44 << 20),
        cost_estimate=pl.CostEstimate(
            flops=12 * rows * hid * total, bytes_accessed=12 * hid * total, transcendentals=0
        ),
        name="experts",
    )(where, *blocks, *extra, *weights)


def added(a, b):
    return a.astype(jnp.float32) + b.astype(jnp.float32)


def tied(value, *others):
    return lax.optimization_barrier((value, others))[0]


def dense_plan(
    queries,
    keys,
    values,
    residual,
    out_projection,
    norm_gain,
    route_ids,
    route_weights,
    w_gate,
    w_up,
    w_down,
):
    tokens = queries.shape[0]
    rows, total = residual.shape
    columns = out_projection.shape[1]
    spare = -columns % 128
    experts = lax.axis_size("ctx") * lax.axis_size("head")
    z, e, h = lax.axis_index("ctx"), lax.axis_index("exp"), lax.axis_index("head")
    i32 = jnp.int32

    prior_k = from_behind(keys, ("ctx", "exp"), 1)
    prior_v = from_behind(values, ("ctx", "exp"), 1)
    w_own = out_projection.T
    w_partner = swapped(w_own, "head", 1)

    me = e[None].astype(i32)
    rests = pack(me, residual, route_ids, route_weights, columns, columns + spare, experts)
    ready = rests[1:]
    rests = [rests[0]] + [swapped(rests[s], "exp", s) for s in range(1, 4)]
    gain = lax.dynamic_slice_in_dim(norm_gain, e * columns, columns, 0)
    gain = jnp.pad(gain, (0, spare), constant_values=1.0)[None, :]

    place = jnp.stack([(z * 4 + e) * tokens, h]).astype(i32)
    mine, other = attention(tied(place, ready), queries, prior_k, keys, prior_v, values)
    mine, other = tied((mine, other), rests)
    theirs = swapped(other, "head", 1)
    mine = [mine] + [swapped(mine, "exp", s) for s in (3, 1, 2)]
    theirs = [theirs] + [swapped(theirs, "exp", s) for s in (3, 1, 2)]
    mine, theirs = [[a[0], a[2], a[3], a[1]] for a in (mine, theirs)]
    block, attn = project(me, mine, theirs, rests, w_own, w_partner, gain)
    mats = [w_gate[0], w_up[0], w_down[0].T]
    weights = mats + [swapped(tied(m, block), "head", 1) for m in mats]

    where = jnp.stack([e, z * 2 + h, z * 2 + 1 - h]).astype(i32)
    planes = lax.axis_size("ctx")
    part = rows // 2
    arrived, gathered, outs, sums = {0: block}, {}, {}, {}

    def begin_gather(s):
        first, second = (1, 2) if s % 2 == 0 else (2, 1)
        v = arrived[s]
        a, b = swapped(v, "exp", first), swapped(v, "exp", second)
        c = swapped(a, "exp", second)
        gathered[s] = (v, a, b, c) if first == 1 else (v, b, a, c)

    def compute(s, *after):
        outs[s] = expert_chunk(
            tied(where, *after), gathered[s], weights, attn if s == 0 else None, columns, experts
        )

    def reduce(s):
        own, keep, sx, sy = outs[s]
        gx = swapped(sx, "exp", 1)
        gy = swapped(sy, "exp", 2)
        fy = swapped(added(keep[:part], gx[part:]).astype(jnp.bfloat16), "exp", 2)
        fx = swapped(added(keep[part:], gy[part:]).astype(jnp.bfloat16), "exp", 1)
        sums[s] = own, gx, gy, fx, fy

    begin_gather(0)
    for s in range(1, planes):
        arrived[s] = swapped(tied(block, arrived[s - 1]) if s > 1 else block, "ctx", s)
        if s > 1:
            arrived[s] = tied(arrived[s], outs[s - 2][2])
        begin_gather(s)
        compute(s - 1, *([outs[s - 2][2]] if s > 1 else []))
        if s > 1:
            reduce(s - 1)
    compute(planes - 1, outs[planes - 2][2])
    reduce(planes - 1)
    outs[0] = tied(outs[0], outs[planes - 1][2])
    reduce(0)

    def joined(own, gx, gy, fx, fy, *more):
        halves = []
        for begin, g, f in ((0, gx, fy), (part, gy, fx)):
            half = added(added(own[begin : begin + part], g[:part]), f)
            for other in more:
                half = added(half, other[begin : begin + part])
            halves.append(half.astype(jnp.bfloat16))
        return jnp.concatenate(halves, axis=0)

    backs = [swapped(joined(*sums[s]), "ctx", s) for s in range(1, planes)]
    return joined(*sums[0], residual, *backs)


def local(*arrays):
    queries, out_projection, residual = arrays[0], arrays[4], arrays[3]
    tokens = queries.shape[0]
    planes, heads = lax.axis_size("ctx"), lax.axis_size("head")
    experts = planes * heads
    rows = residual.shape[0]
    spare = -out_projection.shape[1] % 128
    dense = (
        max(2, TOP * tokens // experts) >= rows
        and heads == 2
        and lax.axis_size("exp") == 4
        and planes & (planes - 1) == 0
        and tokens == BAND_WIDTH_KEYS
        and 2 + 2 * experts <= spare
    )
    return (dense_plan if dense else sparse_plan)(*arrays)


def solution(mesh):
    return jax.shard_map(
        local,
        mesh=mesh,
        in_specs=(
            P(("ctx", "exp"), "head"),
            P(("ctx", "exp"), "head"),
            P(("ctx", "exp"), "head"),
            P(("ctx", "exp", "head"), None),
            P("head", "exp"),
            P(),
            P(("ctx", "exp", "head"), None),
            P(("ctx", "exp", "head"), None),
            P(("ctx", "head"), None, "exp"),
            P(("ctx", "head"), None, "exp"),
            P(("ctx", "head"), "exp", None),
        ),
        out_specs=P(("ctx", "exp", "head"), None),
        check_vma=False,
    )
```
